256 devices in a mesh: row: 16 (over z_lo, y), col: 4 (over x), sta: 4 (over z_hi, core).
Axes of the slice: x: 4, y: 4, z: 8 (z_hi: 2, z_lo: 4; z = z_hi * 4 + z_lo), core: 2. Of those that a mesh axis runs over, the one named last changes fastest.
Arguments:
- templates: float32 [4096, 12, 3, 256], P(('row', 'col'), 'sta'), may hold values from -40 to 40
- avail: int32 [4096, 12], P(('row', 'col')), may hold values 0 or 1
- labels: int32 [4096], P(('row', 'col')), may hold values from 0 to 511, as said below
- owner_slot: int32 [512], replicated, may hold values from 0 to 511, as said below
Outputs:
- similarity: float32 [64, 4, 16, 4096], P('sta', 'col', None, 'row')
- stacks: float32 [512, 12, 3, 256], P(('row', 'col'), 'sta')
The draws below stay inside these ranges and needn't reach their ends.
Inputs may be any that keep to these rules, and one draw needn't show every extreme that they name: `labels`: the owner of cluster k is owner_slot[k] // 8; among the 64 templates of each aligned block (one row and column index, blocks in order of row then col) at most 2 name clusters of one owner, and one owner gets exactly 2 from every block. `owner_slot`: each slot 0 .. 511 appears once.
All inputs are finite; a program needn't handle non-finite values. No bound on the sum of `avail` on one device may be relied on, other than what follows from the above.
Results may differ from the reference program's by a relative error of at most 0.006.
Values may be sent and summed in bfloat16 or wider, within the bound.
No kernel may reach another device: no remote copies, remote signals or barrier semaphores. Data moves between devices by JAX's collectives and lax.ppermute only.
A program may use at most 64 MiB of HBM per device.

```python
import jax
import jax.numpy as jnp
from jax import lax

NST = 12
NCOMP = 3
NT = 256
MAXLAG = 4
CLO = 8
SHARD = 64
OWNERS = 64
M = 4096
NCL = 512
CAP = 2
N_ROW = 16
N_COL = 4
N_STA = 4


def label_parts(key):
    holder_list = OWNERS
    owner_slot = jax.random.permutation(jax.random.fold_in(key, 101), jnp.arange(NCL, dtype=jnp.int32))
    hot = max(1, SHARD // (4 * CAP))
    holder_position = jax.random.permutation(jax.random.fold_in(key, 102), jnp.arange(holder_list, dtype=jnp.int32))
    extra_reward = jnp.where(holder_position == 0, 1 << 16, jnp.where(holder_position < holder_list // 4, 1 << 13, 0))
    random_jitter = jax.random.randint(jax.random.fold_in(key, 103), (holder_list, holder_list), 0, 1 << 12)
    match_rating = (random_jitter + extra_reward[None, :]) * 256 + jnp.arange(holder_list, dtype=jnp.int32)[None, :]
    order = jnp.argsort(-match_rating, axis=1).astype(jnp.int32)
    position = jnp.arange(SHARD, dtype=jnp.int32)
    column = jnp.where(position < CAP * hot, position // CAP, hot + (position - CAP * hot) % (holder_list - hot))
    owner = jnp.take_along_axis(order, jnp.broadcast_to(column[None, :], (holder_list, SHARD)), axis=1)
    within = jax.random.randint(jax.random.fold_in(key, 104), (holder_list, SHARD), 0, CLO)
    slot = owner * CLO + within
    inverse = jnp.zeros((NCL,), jnp.int32).at[owner_slot].set(jnp.arange(NCL, dtype=jnp.int32))
    labels = inverse[slot.reshape(M)]
    return (owner_slot, labels)


def draw_owner_slot(key, part):
    return label_parts(key)[0]


def draw_labels(key, part):
    return label_parts(key)[1]


def draw_templates(key, part):
    labels = label_parts(key)[1]
    proto = jax.random.normal(jax.random.fold_in(key, 201), (NCL, NST, NCOMP, NT), jnp.float32)
    delay = jax.random.randint(jax.random.fold_in(key, 202), (M,), -3, 4)
    index = (jnp.arange(NT, dtype=jnp.int32)[None, :] - delay[:, None]) % NT
    base = proto[labels]
    base = jnp.take_along_axis(base, jnp.broadcast_to(index[:, None, None, :], base.shape), axis=3)
    shape = (M, NST, NCOMP, NT)
    random_jitter = jax.random.normal(jax.random.fold_in(key, 203), shape, jnp.float32)
    level = jax.random.uniform(jax.random.fold_in(key, 204), (M, NST), jnp.float32, jnp.log(0.3), jnp.log(3.0))
    values = jnp.exp(level)[:, :, None, None] * (0.8 * base + 0.6 * random_jitter)
    return jnp.clip(values, -40.0, 40.0).astype(jnp.float32)


def plant(entries, own_key, smallest, top_value):
    index_at = [jax.random.randint(jax.random.fold_in(own_key, axis), (), 0, length) for axis, length in enumerate(entries.shape)]
    main_axis = entries.shape.index(max(entries.shape))
    neighbour = index_at[:main_axis] + [(index_at[main_axis] + 1) % entries.shape[main_axis]] + index_at[main_axis + 1:]
    return entries.at[tuple(index_at)].set(smallest).at[tuple(neighbour)].set(top_value)


def setup_inputs(seed: int = 0) -> dict:
    key_list = jax.random.split(jax.random.key(seed), 5)
    templates = draw_templates(jax.random.fold_in(key_list[4], 71), 0)
    avail = plant((jax.random.randint(key_list[1], (M, NST), 0, 2) < 1).astype(jnp.int32), jax.random.fold_in(key_list[1], 1), 0, 1)
    labels = draw_labels(jax.random.fold_in(key_list[4], 71), 0)
    owner_slot = draw_owner_slot(jax.random.fold_in(key_list[4], 71), 0)
    return {"templates": templates, "avail": avail, "labels": labels, "owner_slot": owner_slot}


EPS = 1e-06

def unit_rms(templates, present):
    mean_sq = lax.optimization_barrier(jnp.mean(templates * templates, axis=(2, 3), keepdims=True))
    scaled = templates * lax.rsqrt(mean_sq + EPS)
    return (scaled * present[:, :, None, None].astype(jnp.float32)).astype(jnp.bfloat16)

def reference(templates, avail, labels, owner_slot):
    waves = unit_rms(templates, avail)
    lags = 2 * MAXLAG + 1
    span = NST // N_STA
    width = span * NCOMP * NT
    rows = waves.reshape(M, N_STA, width).astype(jnp.float32)
    padded = jnp.pad(waves, ((0, 0), (0, 0), (0, 0), (MAXLAG, MAXLAG)))

    def column_block(index):
        block = lax.dynamic_slice_in_dim(padded, index * SHARD, SHARD, 0)
        lagged = jnp.stack([block[..., lag:lag + NT] for lag in range(lags)], axis=1)
        lagged = lagged.reshape(SHARD * lags, N_STA, width).astype(jnp.float32)
        total = jnp.zeros((SHARD * lags, M), jnp.float32)
        for group in range(N_STA):
            term = jnp.dot(lagged[:, group], rows[:, group].T, preferred_element_type=jnp.float32)
            term = lax.optimization_barrier(term.astype(jnp.bfloat16))
            total = total + term.astype(jnp.float32)
        return lax.optimization_barrier(jnp.max(total.reshape(SHARD, lags, M), axis=1))
    best = lax.map(column_block, jnp.arange(M // SHARD, dtype=jnp.int32)).reshape(M, M)
    availf = avail.astype(jnp.float32)
    shared = jnp.dot(availf, availf.T, preferred_element_type=jnp.float32)
    similarity = best / (NCOMP * NT * jnp.maximum(shared, 1.0))
    similarity = similarity.reshape(N_ROW, N_COL, SHARD, M).transpose(2, 1, 0, 3)
    slot = owner_slot[labels]
    flat = waves.reshape(M, NST, NCOMP * NT).astype(jnp.float32)
    sums = jax.ops.segment_sum(flat, slot, num_segments=NCL)
    counts = jax.ops.segment_sum(availf, slot, num_segments=NCL)
    stacks = sums / jnp.maximum(counts, 1.0)[:, :, None]
    return (similarity, stacks.reshape(NCL, NST, NCOMP, NT))
```

```python
import jax
import jax.numpy as jnp
from jax import lax
from jax.experimental import pallas as pl
from jax.experimental.pallas import tpu as pltpu
from jax.sharding import PartitionSpec as P

MAXLAG = 4
LAGS = 2 * MAXLAG + 1
EPS = 1e-06
AXES = ("row", "col", "sta")
F32 = jnp.float32
BF16 = jnp.bfloat16


def perm_of(move):
    pairs = []
    for zl in range(4):
        for y in range(4):
            for x in range(4):
                for zh in range(2):
                    for core in range(2):
                        x2, y2, z2, c2 = move(x, y, zh * 4 + zl, core)
                        x2, y2, z2 = x2 % 4, y2 % 4, z2 % 8
                        src = ((zl * 4 + y) * 4 + x) * 4 + zh * 2 + core
                        dst = (((z2 % 4) * 4 + y2) * 4 + x2) * 4 + (z2 // 4) * 2 + c2
                        pairs.append((src, dst))
    return pairs


def from_x(a, d):
    return lax.ppermute(a, AXES, perm_of(lambda x, y, z, c: (x - d, y, z, c)))


def from_y(a, d):
    return lax.ppermute(a, AXES, perm_of(lambda x, y, z, c: (x, y - d, z, c)))


def from_z(a, d):
    return lax.ppermute(a, AXES, perm_of(lambda x, y, z, c: (x, y, z - d, c)))


def to_zlo(a, d):
    return lax.ppermute(
        a, AXES, perm_of(lambda x, y, z, c: (x, y, (z // 4) * 4 + (z % 4 + d) % 4, c))
    )


def from_core(a):
    return lax.ppermute(a, AXES, perm_of(lambda x, y, z, c: (x, y, z, 1 - c)))


def call(body, outs, *args, flops=0, moved=0, scratch=()):
    return pl.pallas_call(
        body,
        out_shape=outs,
        in_specs=[
            pl.BlockSpec(memory_space=pltpu.SMEM if i == 0 else pltpu.VMEM)
            for i in range(len(args))
        ],
        out_specs=jax.tree.map(lambda _: pl.BlockSpec(memory_space=pltpu.VMEM), outs),
        scratch_shapes=list(scratch),
        cost_estimate=pl.CostEstimate(flops=flops, bytes_accessed=moved, transcendentals=0),
    )(*args)


def shape(dims, dtype=BF16):
    return jax.ShapeDtypeStruct(dims, dtype)


def waves_body(pos, tp, avail, labels, slots, unit, other, mine):
    zhi, core = pos[3], pos[4]
    have = avail[...]
    lane = lax.broadcasted_iota(jnp.int32, have.shape, 1)
    for s in range(3):
        x = [tp[3 * s + c] for c in range(3)]
        total = jnp.sum(x[0] * x[0] + x[1] * x[1] + x[2] * x[2], axis=1, keepdims=True)
        scale = lax.rsqrt(total / 768.0 + EPS)
        station = (zhi * 2 + core) * 3 + s
        present = jnp.sum(jnp.where(lane == station, have, 0.0), axis=1, keepdims=True)
        for c in range(3):
            unit[3 * s + c] = (x[c] * scale * present).astype(BF16)
    cluster = lax.broadcasted_iota(jnp.int32, (64, 512), 1)
    slot = jnp.sum(jnp.where(labels[...] == cluster, slots[...], 0), axis=1, keepdims=True)
    owner = (slot // 8).astype(F32)
    which = (slot % 8).astype(F32)
    meta = jnp.where(lane == 12, owner, jnp.where(lane == 13, which, have))
    unit[9] = meta.astype(BF16)
    keep = pl.multiple_of(zhi * 32, 32)
    give = pl.multiple_of((1 - zhi) * 32, 32)
    for p in range(9):
        other[p] = unit[p, pl.ds(give, 32), :]
    for p in range(10):
        mine[p] = unit[p, pl.ds(keep, 32), :]


def rows_body(pos, u0, p1, p2, p3, p4, m1, m2, m3, m4, out):
    zlo, zhi, core = pos[2], pos[3], pos[4]

    def put(plane, d, block, src_plane):
        for cr in range(2):
            for zr in range(2):
                start = pl.multiple_of((zhi ^ zr) * 32 + (core ^ cr) * 16, 16)
                row = (cr * 2 + zr) * 64 + d * 16
                out[plane, row : row + 16, :] = block[src_plane, pl.ds(start, 16), :]

    for p in range(9):
        put(p, 0, u0, p)
        if p < 5:
            put(10 + p, 0, p4, p)
        else:
            put(10 + p, 0, m4, p - 5)
    put(9, 0, u0, 9)
    for d, near, far in ((1, p1, m3), (2, p2, m2), (3, p3, m1)):

        @pl.when(zlo + d < 4)
        def _():
            for p in range(9):
                put(p, d, near, p)
                put(10 + p, d, far, p)

        @pl.when(zlo + d >= 4)
        def _():
            for p in range(9):
                put(p, d, far, p)
                put(10 + p, d, near, p)

        put(9, d, near, 9)


def columns(blocks, plane):
    return jnp.concatenate([ref[q, plane] for ref in blocks for q in range(4)], axis=0)


PLANES = [p for p in range(19) if p != 9]


def corr_body(pos, rows, *refs):
    blocks, (keep, give), (lhs,) = refs[:8], refs[8:10], refs[10:]
    for n, p in enumerate(PLANES):
        lhs[:, n * 256 : (n + 1) * 256] = columns(blocks, p)
    source = lax.broadcasted_iota(jnp.int32, (256, 256), 0)
    target = lax.broadcasted_iota(jnp.int32, (256, 256), 1)

    @pl.loop(0, LAGS)
    def _(lag):
        table = (source == target + (lag - MAXLAG)).astype(F32).astype(BF16)
        rhs = jnp.concatenate(
            [
                jnp.dot(rows[p], table, preferred_element_type=F32).astype(BF16)
                for p in PLANES
            ],
            axis=1,
        )
        got = lax.dot_general(
            lhs[...], rhs, (((1,), (1,)), ((), ())), preferred_element_type=F32
        ).astype(BF16)
        keep[lag] = got[:, :128]
        give[lag] = got[:, 128:]


def avail_only(block):
    lane = lax.broadcasted_iota(jnp.int32, block.shape, 1)
    return jnp.where(lane < 12, block.astype(F32), 0.0).astype(BF16)


def best_body(pos, rows, keep, recv, *refs):
    blocks, (keep_out, give_out) = refs[:8], refs[8:]
    best = keep[0].astype(F32) + recv[0].astype(F32)
    for lag in range(1, LAGS):
        best = jnp.maximum(best, keep[lag].astype(F32) + recv[lag].astype(F32))
    shared = lax.dot_general(
        avail_only(columns(blocks, 9)),
        avail_only(rows[9, :128, :]),
        (((1,), (1,)), ((), ())),
        preferred_element_type=F32,
    )
    sim = (best / (768.0 * jnp.maximum(shared, 1.0))).astype(BF16)
    keep_out[...] = sim[:, :64]
    give_out[...] = sim[:, 64:]


def order_body(pos, kept, got, *outs):
    b = lax.broadcasted_iota(jnp.int32, (512, 128), 0)
    lane = lax.broadcasted_iota(jnp.int32, (512, 128), 1)
    half, k = b // 256, b % 16
    first, second = (b // 64) % 4, (b // 16) % 4
    dy = jnp.where(half == 0, first, second)
    dx = jnp.where(half == 0, second, first)
    at = dx * 32 + half * 16 + k
    for d in range(4):
        table = ((dy == d) & (at == lane)).astype(F32).astype(BF16)
        for n, ref in enumerate((kept, got)):
            outs[d][n] = lax.dot_general(
                ref[...], table, (((0,), (0,)), ((), ())), preferred_element_type=F32
            ).astype(BF16)


def place_body(pos, r0, r1, r2, r3, out):
    x, y, zlo, zhi = pos[0], pos[1], pos[2], pos[3]
    src = lax.broadcasted_iota(jnp.int32, (256, 256), 0)
    dst = lax.broadcasted_iota(jnp.int32, (256, 256), 1)
    col = (src // 32) % 4
    goes = ((x + col) % 4) * 64 + ((src // 128) ^ zhi) * 32 + src % 32
    table = (goes == dst).astype(F32).astype(BF16)
    for d, ref in enumerate((r0, r1, r2, r3)):
        both = jnp.concatenate([ref[0], ref[1]], axis=1)
        moved = jnp.dot(both, table, preferred_element_type=F32)
        for q in range(4):
            r = ((zlo + q) % 4) * 4 + (y + 4 - d) % 4
            out[:, pl.ds(r, 1), :] = moved[q * 16 : q * 16 + 16, :].reshape(16, 1, 256)


def sums_body(pos, *refs):
    blocks, (own, far) = refs[:8], refs[8:]
    x, y, zlo = pos[0], pos[1], pos[2]
    meta = columns(blocks, 9).astype(F32)
    lane = lax.broadcasted_iota(jnp.int32, meta.shape, 1)
    owner = jnp.sum(jnp.where(lane == 12, meta, 0.0), axis=1, keepdims=True)
    which = jnp.sum(jnp.where(lane == 13, meta, 0.0), axis=1, keepdims=True)
    want = lax.broadcasted_iota(jnp.int32, (512, 32), 1)
    want_owner = ((((zlo + want // 8) % 4) * 4 + y) * 4 + x).astype(F32)
    pick = (owner == want_owner) & (which == (want % 8).astype(F32))
    pick = pick.astype(F32).astype(BF16)

    def total(plane):
        return lax.dot_general(
            pick, columns(blocks, plane), (((0,), (0,)), ((), ())), preferred_element_type=F32
        )

    for p in range(9):
        own[p] = total(p)
        far[p] = total(10 + p).astype(BF16)
    counts = total(9)
    own[9] = counts
    far[9] = counts.astype(BF16)


def split_body(pos, own, got, mine, a, b, c):
    for p in range(10):
        whole = own[p] + got[p].astype(F32)
        mine[p] = whole[:8]
        a[p] = whole[8:16].astype(BF16)
        b[p] = whole[16:24].astype(BF16)
        c[p] = whole[24:].astype(BF16)


def stack_body(pos, mine, a, b, c, out):
    zhi, core = pos[3], pos[4]
    counts = mine[9] + a[9].astype(F32) + b[9].astype(F32) + c[9].astype(F32)
    lane = lax.broadcasted_iota(jnp.int32, counts.shape, 1)
    for s in range(3):
        station = (zhi * 2 + core) * 3 + s
        n = jnp.sum(jnp.where(lane == station, counts, 0.0), axis=1, keepdims=True)
        n = jnp.maximum(n, 1.0)
        for p in range(3 * s, 3 * s + 3):
            whole = mine[p] + a[p].astype(F32) + b[p].astype(F32) + c[p].astype(F32)
            out[p] = whole / n


def local(templates, avail, labels, owner_slot):
    row, sta = lax.axis_index("row"), lax.axis_index("sta")
    pos = jnp.stack([lax.axis_index("col"), row % 4, row // 4, sta // 2, sta % 2])
    tp = templates.transpose(1, 2, 0, 3).reshape(9, 64, 256)
    have = jnp.pad(avail.astype(F32), ((0, 0), (0, 244)))
    unit, other, mine = call(
        waves_body,
        (shape((10, 64, 256)), shape((9, 32, 256)), shape((10, 32, 256))),
        pos,
        tp,
        have,
        labels.reshape(64, 1),
        owner_slot.reshape(1, 512),
        moved=1 << 20,
    )
    far = from_z(other, 4)
    p1, m1 = from_z(unit, 1), from_z(unit, -1)
    item = jnp.concatenate([mine, far], axis=0)
    item_a, item_b = item[:, :16], item[:, 16:]
    xa = jnp.stack([item_a] + [from_x(item_a, d) for d in (1, 2, 3)])
    yb = jnp.stack([item_b] + [from_y(item_b, d) for d in (1, 2, 3)])
    p2, m2 = from_z(p1, 1), from_z(m1, -1)
    blocks = (
        [xa]
        + [from_y(xa, d) for d in (1, 2, 3)]
        + [yb]
        + [from_x(yb, d) for d in (1, 2, 3)]
    )
    p3, m3 = from_z(p2, 1), from_z(m2, -1)
    p4, m4 = from_z(p3[:5], 1), from_z(m3[5:9], -1)
    rows = call(
        rows_body, shape((19, 256, 256)), pos, unit, p1, p2, p3, p4, m1, m2, m3, m4, moved=5 << 20
    )
    keep, give = call(
        corr_body,
        (shape((LAGS, 512, 128)), shape((LAGS, 512, 128))),
        pos,
        rows,
        *blocks,
        flops=2 * 512 * 256 * 4608 * LAGS,
        moved=12 << 20,
        scratch=(pltpu.VMEM((512, 4608), BF16),),
    )
    recv = from_core(give)
    sim_keep, sim_give = call(
        best_body, (shape((512, 64)), shape((512, 64))), pos, rows, keep, recv, *blocks, moved=5 << 20
    )
    sim_got = from_z(sim_give, 4)
    parts = call(
        order_body, tuple(shape((2, 64, 128)) for _ in range(4)), pos, sim_keep, sim_got, moved=1 << 18
    )
    placed = [parts[0]] + [from_y(parts[d], -d) for d in (1, 2, 3)]
    similarity = call(place_body, shape((16, 16, 256), F32), pos, *placed, moved=1 << 19)
    own, far_sums = call(
        sums_body, (shape((10, 32, 256), F32), shape((10, 32, 256))), pos, *blocks, moved=5 << 20
    )
    got_sums = from_z(far_sums, 4)
    quarter = shape((10, 8, 256))
    here, *away = call(
        split_body,
        (shape((10, 8, 256), F32), quarter, quarter, quarter),
        pos,
        own,
        got_sums,
        moved=1 << 19,
    )
    came = [to_zlo(a, d) for d, a in zip((1, 2, 3), away)]
    stacks = call(stack_body, shape((9, 8, 256), F32), pos, here, *came, moved=1 << 18)
    stacks = stacks.reshape(3, 3, 8, 256).transpose(2, 0, 1, 3)
    return similarity.reshape(16, 1, 16, 256), stacks


def solution(mesh):
    in_specs = (
        P(("row", "col"), "sta", None, None),
        P(("row", "col"), None),
        P(("row", "col")),
        P(),
    )
    out_specs = (P("sta", "col", None, "row"), P(("row", "col"), "sta", None, None))
    return jax.shard_map(local, mesh=mesh, in_specs=in_specs, out_specs=out_specs, check_vma=False)
```
